512 devices in a mesh: dom: 128 (over z, y, core), rep: 4 (over x).
Axes of the slice: x: 4, y: 4, z: 16, core: 2. Of those that a mesh axis runs over, the one named last changes fastest.
Arguments:
- profiles: bfloat16 [300, 131072], P(None, 'dom'), may hold values from -6 to 6
- pack_index: int32 [128, 4, 128, 16], P('dom', 'rep'), may hold values from 0 to 1023, as said below
- obs_slot: int32 [4, 262144], P(None, ('dom', 'rep')), may hold values from 0 to 2047, as said below
- interp_weight: float32 [4, 262144], P(None, ('dom', 'rep')), may hold values from 0 to 1, as said below
- departures: float32 [100, 262144], P(None, ('dom', 'rep')), may hold values from -6 to 6
- w_in: bfloat16 [300, 512], replicated, may hold values from -0.375 to 0.375
- b_in: float32 [512], replicated, may hold values from -4 to 4
- w_mid: bfloat16 [512, 512], replicated, may hold values from -0.25 to 0.25
- b_mid: float32 [512], replicated, may hold values from -4 to 4
- w_out: bfloat16 [512, 100], replicated, may hold values from -0.25 to 0.25
Outputs:
- column_adjoint: float32 [300, 131072], P(None, ('dom', 'rep'))
The draws below stay inside these ranges and needn't reach their ends.
Inputs may be any that keep to these rules, and one draw needn't show every extreme that they name: Local column numbers within the partition that holds pack_index's first index; the 16 columns of pack_index[o, r, d, :] are distinct and lie in quarter d % 4 of the partition, that is from (d % 4) * 256 to one less than (d % 4 + 1) * 256. `obs_slot`: slot o * 16 + j names the j-th column that the observation's segment and replica index take from partition o; where o lies more than 2 partitions from the segment's own index, counted cyclically, j < 4. `interp_weight`: bilinear weights: the four of an observation sum to one.
All inputs are finite; a program needn't handle non-finite values.
Results may differ from the reference program's by a relative error of at most 0.0057.
Values may be sent and summed in bfloat16 or wider, within the bound.
No kernel may reach another device: no remote copies, remote signals or barrier semaphores. Data moves between devices by JAX's collectives and lax.ppermute only.
A program may use at most 64 MiB of HBM per device.

```python
import jax
import jax.numpy as jnp
from jax import lax

F = 300
H = 512
C = 100
COL_DEV = 1024
OBS_DEV = 512
CAP = 16
NEAR = 2
FAR = 4
NCOL = 131072
NOBS = 262144
N_DOM = 128
N_REP = 4


def draw_pack_index(key, part):
    key_base = jax.random.fold_in(key, 11)
    key_order = jax.random.fold_in(key, 12)
    quarter = COL_DEV // N_REP
    base = jax.random.randint(key_base, (N_DOM, N_REP, N_DOM, 1), 0, quarter)
    scores = jax.random.randint(key_order, (N_DOM, N_REP, N_DOM, CAP), 0, 65536) * CAP + jnp.arange(CAP, dtype=jnp.int32)
    order = jnp.argsort(scores, axis=-1, stable=True).astype(jnp.int32)
    segment_quarter = (jnp.arange(N_DOM, dtype=jnp.int32) % N_REP).reshape(1, 1, N_DOM, 1)
    return ((base + order) % quarter + segment_quarter * quarter).astype(jnp.int32)


def draw_obs_slot(key, part):
    obs_index = jnp.arange(NOBS, dtype=jnp.int32)
    segment = obs_index // OBS_DEV // N_REP
    home_offset = jax.random.randint(jax.random.fold_in(key, 21), (NOBS,), -NEAR, NEAR + 1)
    choose = jax.random.randint(jax.random.fold_in(key, 22), (4, NOBS), 0, 2)
    far_owner = jax.random.randint(jax.random.fold_in(key, 23), (4, NOBS), 0, N_DOM)
    near_owner = (segment + home_offset) % N_DOM
    owner_index = jnp.where(choose == 0, near_owner[None, :], far_owner)
    apart = (owner_index - segment[None, :]) % N_DOM
    distance = jnp.minimum(apart, N_DOM - apart)
    limit = jnp.where(distance <= NEAR, CAP, FAR)
    within = jax.random.randint(jax.random.fold_in(key, 24), (4, NOBS), 0, 1048576) % limit
    return (owner_index * CAP + within).astype(jnp.int32)


def draw_interp_weight(key, part):
    key_east = jax.random.fold_in(key, 31)
    key_north = jax.random.fold_in(key, 32)
    east = jax.random.uniform(key_east, (NOBS,), jnp.float32, 0.05, 0.95)
    north = jax.random.uniform(key_north, (NOBS,), jnp.float32, 0.05, 0.95)
    stacked = jnp.stack([(1.0 - east) * (1.0 - north), east * (1.0 - north), (1.0 - east) * north, east * north])
    return stacked.astype(jnp.float32)


def shard_levels(rng, shape, shards, smallest, top_value):
    def one(position, blocks):
        draws = jax.random.uniform(jax.random.fold_in(jax.random.fold_in(rng, 6), position), (blocks,), jnp.float32, smallest / len(shards), top_value / len(shards))
        return jnp.repeat(jnp.exp(draws), shape[position] // blocks).reshape((-1,) + (1,) * (len(shape) - position - 1))

    gain = one(*shards[0])
    for cut in shards[1:]:
        gain = gain * one(*cut)
    return gain


def noise(own_key, extent, scale, bound, shards=(), kind=jnp.bfloat16):
    loudness = shard_levels(own_key, extent, shards, -0.22, 0.18) if shards else 1.0
    array = jax.random.normal(own_key, extent, jnp.float32) * scale * loudness
    return jnp.minimum(jnp.maximum(array, -bound), bound).astype(kind)


def setup_inputs(seed: int = 0) -> dict:
    key_list = jax.random.split(jax.random.key(seed), 11)
    profiles = noise(key_list[0], (F, NCOL), 1.0, 6.0, ((1, 128),))
    pack_index = draw_pack_index(jax.random.fold_in(key_list[10], 71), 0)
    obs_slot = draw_obs_slot(jax.random.fold_in(key_list[10], 71), 0)
    interp_weight = draw_interp_weight(jax.random.fold_in(key_list[10], 71), 0)
    departures = noise(key_list[4], (C, NOBS), 1.0, 6.0, ((1, 512),), jnp.float32)
    w_in = noise(key_list[5], (F, H), F ** -0.5, 0.375)
    b_in = noise(key_list[6], (H,), 1.0, 4.0, (), jnp.float32)
    w_mid = noise(key_list[7], (H, H), H ** -0.5, 0.25)
    b_mid = noise(key_list[8], (H,), 1.0, 4.0, (), jnp.float32)
    w_out = noise(key_list[9], (H, C), H ** -0.5, 0.25)
    return dict(profiles=profiles, pack_index=pack_index, obs_slot=obs_slot, interp_weight=interp_weight, departures=departures, w_in=w_in, b_in=b_in, w_mid=w_mid, b_mid=b_mid, w_out=w_out)


def stencil_columns(pack_index, obs_slot):
    obs_index = jnp.arange(NOBS, dtype=jnp.int32)
    device_index = obs_index // OBS_DEV
    segment = device_index // N_REP
    replica = device_index % N_REP
    owner_index = obs_slot // CAP
    within = obs_slot % CAP
    local_column = pack_index[owner_index, replica[None, :], segment[None, :], within]
    return (owner_index * COL_DEV + local_column).astype(jnp.int32)


def reference(profiles, pack_index, obs_slot, interp_weight, departures, w_in, b_in, w_mid, b_mid, w_out):
    column = stencil_columns(pack_index, obs_slot)
    block_count = NOBS // OBS_DEV
    column_blocks = column.reshape(4, block_count, OBS_DEV).transpose(1, 0, 2)
    weight_blocks = interp_weight.reshape(4, block_count, OBS_DEV).transpose(1, 0, 2)
    depart_blocks = departures.reshape(C, block_count, OBS_DEV).transpose(1, 0, 2)

    def advance(adjoint, block):
        columns_used, weights_used, depart_used = block
        summed = jnp.zeros((F, OBS_DEV), jnp.float32)
        for corner in range(4):
            summed = summed + weights_used[corner] * profiles[:, columns_used[corner]].astype(jnp.float32)
        inputs = summed.astype(jnp.bfloat16)
        z_one = jnp.dot(w_in.T, inputs, preferred_element_type=jnp.float32) + b_in[:, None]
        act_one = jnp.tanh(z_one).astype(jnp.bfloat16)
        z_two = jnp.dot(w_mid.T, act_one, preferred_element_type=jnp.float32) + b_mid[:, None]
        cot_out = depart_used.astype(jnp.bfloat16)
        g_two = (jnp.dot(w_out, cot_out, preferred_element_type=jnp.float32) * (1.0 - jnp.tanh(z_two) ** 2)).astype(jnp.bfloat16)
        g_one = (jnp.dot(w_mid, g_two, preferred_element_type=jnp.float32) * (1.0 - jnp.tanh(z_one) ** 2)).astype(jnp.bfloat16)
        g_inputs = jnp.dot(w_in, g_one, preferred_element_type=jnp.float32)
        for corner in range(4):
            adjoint = adjoint.at[:, columns_used[corner]].add(weights_used[corner] * g_inputs)
        return adjoint, None

    adjoint, _ = lax.scan(advance, jnp.zeros((F, NCOL), jnp.float32), (column_blocks, weight_blocks, depart_blocks))
    return adjoint
```

```python
import jax
import jax.numpy as jnp
from jax import lax
from jax.experimental import pallas as pl
from jax.experimental.pallas import tpu as pltpu
from jax.sharding import PartitionSpec as P

F32 = jnp.float32
BF16 = jnp.bfloat16
N_DOM = 128
N_REP = 4
CAP = 16
FAR = 4
REACH = 2
FEAT = 300
WIDE = FEAT + 1
PAIR = 2 * WIDE
FAR_ROWS = N_DOM * FAR // 2
NEAR_ROWS = (CAP - FAR) // 2
NEAR_ALL = (2 * REACH + 1) * NEAR_ROWS
ROWS = 288
QUARTER = 256
COLS = 1024


def dot(a, b, ca, cb):
    return lax.dot_general(a, b, (((ca,), (cb,)), ((), ())), preferred_element_type=F32)


def pack_kernel(idx_ref, prof_ref, far_ref, near_ref):
    prof = prof_ref[...]
    lane = lax.broadcasted_iota(jnp.int32, (ROWS, COLS), 1)
    place = (lax.broadcasted_iota(jnp.int32, (8, COLS), 1) % QUARTER).astype(F32).astype(BF16)
    halves = []
    for p in range(2):
        pick = jnp.where(idx_ref[:, p : p + 1] == lane, 1.0, 0.0).astype(BF16)
        halves.append(dot(pick, prof, 1, 1))
        halves.append(dot(pick, place, 1, 1)[:, :1])
    rows = jnp.concatenate(halves, axis=1).astype(BF16)
    far_ref[...] = rows[:FAR_ROWS]
    near_ref[...] = rows[FAR_ROWS:]


def prep_kernel(
    dom_ref, slot_ref, weight_ref, dep_ref, w_in_ref, w_mid_ref, w_out_ref,
    hi_ref, lo_ref, hi_t_ref, lo_t_ref, seed_ref, w_in_t_ref, w_mid_t_ref,
):
    slot = slot_ref[...]
    owner = slot // CAP
    j = slot % CAP
    apart = (owner - dom_ref[0] + REACH) % N_DOM
    row = jnp.where(
        j < FAR, owner * (FAR // 2) + j // 2, FAR_ROWS + apart * NEAR_ROWS + (j - FAR) // 2
    )
    obs = slot.shape[1]
    index = lax.broadcasted_iota(jnp.int32, (ROWS, obs), 0)
    for p in range(2):
        mine = jnp.where(j % 2 == p, row, -1)
        acc = jnp.zeros((ROWS, obs), F32)
        for k in range(4):
            acc = acc + jnp.where(mine[k : k + 1] == index, weight_ref[k : k + 1], 0.0)
        hi = acc.astype(BF16)
        lo = acc - hi.astype(F32)
        hi_ref[p] = hi
        lo_ref[p] = lo.astype(BF16)
        hi_t_ref[p] = acc.T.astype(BF16)
        lo_t_ref[p] = lo.T.astype(BF16)
    seed_ref[...] = dot(dep_ref[...].astype(BF16), w_out_ref[...], 0, 1)
    w_in_t_ref[...] = w_in_ref[...].T
    w_mid_t_ref[...] = w_mid_ref[...].T


def main_kernel(
    far_ref, near_ref, hi_ref, lo_ref, hi_t_ref, lo_t_ref, seed_ref,
    w_in_ref, b_in_ref, w_mid_ref, b_mid_ref, w_in_t_ref, w_mid_t_ref,
    far_out_ref, near_out_ref,
):
    fetched = jnp.concatenate([far_ref[...], near_ref[...]], axis=0)
    summed = None
    for p in range(2):
        values = fetched[:, p * WIDE : p * WIDE + FEAT]
        part = dot(hi_t_ref[p], values, 1, 0) + dot(lo_t_ref[p], values, 1, 0)
        summed = part if summed is None else summed + part
    inputs = summed.astype(BF16)
    t_one = jnp.tanh(dot(inputs, w_in_ref[...], 1, 0) + b_in_ref[...])
    t_two = jnp.tanh(dot(t_one.astype(BF16), w_mid_ref[...], 1, 0) + b_mid_ref[...])
    g_two = (seed_ref[...] * (1.0 - t_two * t_two)).astype(BF16)
    g_one = (dot(g_two, w_mid_t_ref[...], 1, 0) * (1.0 - t_one * t_one)).astype(BF16)
    g_inputs = dot(g_one, w_in_t_ref[...], 1, 0)
    g_hi = g_inputs.astype(BF16)
    g_lo = (g_inputs - g_hi.astype(F32)).astype(BF16)
    halves = []
    for p in range(2):
        halves.append(dot(hi_ref[p], g_hi, 1, 0) + dot(lo_ref[p], g_hi, 1, 0) + dot(hi_ref[p], g_lo, 1, 0))
        halves.append(fetched[:, p * WIDE + FEAT : (p + 1) * WIDE].astype(F32))
    rows = jnp.concatenate(halves, axis=1).astype(BF16)
    far_out_ref[...] = rows[:FAR_ROWS]
    near_out_ref[...] = rows[FAR_ROWS:]


def final_kernel(got_ref, out_ref):
    got = got_ref[...]
    lane = lax.broadcasted_iota(jnp.int32, (got.shape[0], QUARTER), 1).astype(F32)
    total = None
    for p in range(2):
        place = got[:, p * WIDE + FEAT : (p + 1) * WIDE].astype(F32)
        pick = jnp.where(place == lane, 1.0, 0.0).astype(BF16)
        part = dot(got[:, p * WIDE : p * WIDE + FEAT], pick, 0, 0)
        total = part if total is None else total + part
    out_ref[...] = total


def shape(dims, dtype):
    return jax.ShapeDtypeStruct(dims, dtype)


def exchange_near(near, sign):
    moved = []
    for i in range(2 * REACH + 1):
        step = sign * (i - REACH)
        block = near[i]
        if step:
            block = lax.ppermute(block, "dom", [(a, (a + step) % N_DOM) for a in range(N_DOM)])
        moved.append(block)
    return moved


def body(
    profiles, pack_index, obs_slot, interp_weight, departures, w_in, b_in, w_mid, b_mid, w_out
):
    dom = lax.axis_index("dom")
    lists = pack_index[0, 0]
    around = jnp.concatenate([lists[-REACH:], lists, lists[:REACH]], axis=0)
    near_lists = lax.dynamic_slice_in_dim(around, dom, 2 * REACH + 1, 0)
    idx = jnp.concatenate(
        [
            lists[:, :FAR].reshape(FAR_ROWS, 2),
            near_lists[:, FAR:].reshape(NEAR_ALL, 2),
            jnp.zeros((ROWS - FAR_ROWS - NEAR_ALL, 2), jnp.int32),
        ],
        axis=0,
    )
    extra = ROWS - FAR_ROWS
    far, near = pl.pallas_call(
        pack_kernel,
        out_shape=(shape((FAR_ROWS, PAIR), BF16), shape((extra, PAIR), BF16)),
        name="pack",
    )(idx, profiles)

    obs = obs_slot.shape[1]
    hidden = w_mid.shape[0]
    smem = pl.BlockSpec(memory_space=pltpu.SMEM)
    vmem = pl.BlockSpec(memory_space=pltpu.VMEM)
    hi, lo, hi_t, lo_t, seed, w_in_t, w_mid_t = pl.pallas_call(
        prep_kernel,
        out_shape=(
            shape((2, ROWS, obs), BF16), shape((2, ROWS, obs), BF16),
            shape((2, obs, ROWS), BF16), shape((2, obs, ROWS), BF16),
            shape((obs, hidden), F32), shape((hidden, FEAT), BF16), shape((hidden, hidden), BF16),
        ),
        in_specs=[smem] + [vmem] * 6,
        name="prep",
    )(dom.reshape(1).astype(jnp.int32), obs_slot, interp_weight, departures, w_in, w_mid, w_out)

    near_parts = near[:NEAR_ALL].reshape(2 * REACH + 1, NEAR_ROWS // 2, 2, PAIR)
    got_near = exchange_near(near_parts, 1)
    got_far = lax.all_to_all(far.reshape(N_DOM, FAR // 2, PAIR), "dom", 0, 0, tiled=True)
    near_rows = jnp.concatenate(got_near[::-1], axis=0).reshape(NEAR_ALL, PAIR)
    near_rows = jnp.pad(near_rows, ((0, extra - NEAR_ALL), (0, 0)))

    far_adj, near_adj = pl.pallas_call(
        main_kernel,
        out_shape=(shape((FAR_ROWS, PAIR), BF16), shape((extra, PAIR), BF16)),
        name="main",
    )(
        got_far.reshape(FAR_ROWS, PAIR), near_rows, hi, lo, hi_t, lo_t, seed,
        w_in, b_in.reshape(1, -1), w_mid, b_mid.reshape(1, -1), w_in_t, w_mid_t,
    )

    near_parts = near_adj[:NEAR_ALL].reshape(2 * REACH + 1, NEAR_ROWS // 2, 2, PAIR)
    back_near = exchange_near(near_parts, 1)[::-1]
    back_far = lax.all_to_all(far_adj.reshape(N_DOM, FAR // 2, PAIR), "dom", 0, 0, tiled=True)
    stacked = jnp.stack(back_near[:N_REP] * 2)
    first = lax.dynamic_slice_in_dim(stacked, (REACH - dom) % N_REP, N_REP, 0)
    owner = (jnp.arange(N_REP) == (dom + REACH) % N_REP).reshape(N_REP, 1, 1, 1)
    second = jnp.where(owner, back_near[N_REP][None], jnp.zeros((), BF16))
    by_quarter = back_far.reshape(N_DOM // N_REP, N_REP, FAR // 2, PAIR).transpose(1, 0, 2, 3)
    outgoing = jnp.concatenate([by_quarter, first, second], axis=1)
    got = lax.all_to_all(outgoing, "rep", 0, 0, tiled=True)
    return pl.pallas_call(
        final_kernel, out_shape=shape((FEAT, QUARTER), F32), name="final"
    )(got.reshape(-1, PAIR))


def solution(mesh):
    placed = (
        P(None, "dom"),
        P("dom", "rep", None, None),
        P(None, ("dom", "rep")),
        P(None, ("dom", "rep")),
        P(None, ("dom", "rep")),
        P(),
        P(),
        P(),
        P(),
        P(),
    )
    return jax.shard_map(
        body, mesh=mesh, in_specs=placed, out_specs=P(None, ("dom", "rep")), check_vma=False
    )
```

```python
import jax
import jax.numpy as jnp
from jax import lax
from jax.experimental import pallas as pl
from jax.experimental.pallas import tpu as pltpu
from jax.sharding import PartitionSpec as P


F32 = jnp.float32
BF16 = jnp.bfloat16
N_DOM = 128
N_REP = 4
CAP = 16
FAR = 4
REACH = 2
FEAT = 300
WIDE = FEAT + 1
PAIR = 2 * WIDE
FAR_ROWS = N_DOM * FAR // 2
NEAR_ROWS = (CAP - FAR) // 2
NEAR_PAD = 32
ROWS = FAR_ROWS + NEAR_PAD
QUARTER = 256
COLS = 1024


def dot(a, b, ca, cb):
    return lax.dot_general(a, b, (((ca,), (cb,)), ((), ())), preferred_element_type=F32)


def pack_kernel(dom_ref, lists_ref, prof_ref, far_ref, near_ref, idx_ref):
    idx = lists_ref[...].T
    idx_ref[...] = idx
    pairs = jnp.broadcast_to(idx[:, None, :], (N_DOM, FAR // 2, CAP)).reshape(FAR_ROWS, CAP)
    first = lax.broadcasted_iota(jnp.int32, (FAR_ROWS, 1), 0) % 2 == 0
    row = lax.broadcasted_iota(jnp.int32, (NEAR_PAD, CAP), 0)
    slot = lax.broadcasted_iota(jnp.int32, (NEAR_PAD, CAP), 1)
    around = jnp.zeros((NEAR_PAD, CAP), jnp.int32)
    for i in range(2 * REACH + 1):
        other = idx_ref[pl.ds((dom_ref[0] + i + N_DOM - REACH) % N_DOM, 1), :]
        around = jnp.where(row // NEAR_ROWS == i, other, around)
    around = around.astype(F32)
    prof = prof_ref[...]
    lane = lax.broadcasted_iota(jnp.int32, (ROWS, COLS), 1)
    halves = []
    for p in range(2):
        near_col = jnp.sum(
            jnp.where(slot == FAR + 2 * (row % NEAR_ROWS) + p, around, 0.0), axis=1, keepdims=True
        ).astype(jnp.int32)
        far_col = jnp.where(first, pairs[:, p : p + 1], pairs[:, 2 + p : 3 + p])
        col = jnp.concatenate([far_col, near_col], axis=0)
        pick = jnp.where(col == lane, 1.0, 0.0).astype(BF16)
        halves.append(dot(pick, prof, 1, 1))
        halves.append((col % QUARTER).astype(F32))
    rows = jnp.concatenate(halves, axis=1).astype(BF16)
    far_ref[...] = rows[:FAR_ROWS].reshape(far_ref.shape)
    near_ref[...] = rows[FAR_ROWS:].reshape(near_ref.shape)


def prep_kernel(
    dom_ref, slot_ref, weight_ref, dep_ref, w_in_ref, w_mid_ref, w_out_ref,
    hi_ref, lo_ref, hi_t_ref, lo_t_ref, seed_ref, w_in_t_ref, w_mid_t_ref,
):
    slot = slot_ref[...]
    owner = slot // CAP
    j = slot % CAP
    apart = (owner - dom_ref[0] + REACH) % N_DOM
    row = jnp.where(
        j < FAR, owner * (FAR // 2) + j // 2, FAR_ROWS + apart * NEAR_ROWS + (j - FAR) // 2
    )
    row = row + ROWS * (j % 2)
    index = lax.broadcasted_iota(jnp.int32, (2 * ROWS, slot.shape[1]), 0)
    acc = jnp.zeros(index.shape, F32)
    for k in range(4):
        acc = acc + jnp.where(row[k : k + 1] == index, weight_ref[k : k + 1], 0.0)
    hi = acc.astype(BF16)
    lo = acc - hi.astype(F32)
    hi_ref[...] = hi
    lo_ref[...] = lo.astype(BF16)
    hi_t_ref[...] = acc.T.astype(BF16)
    lo_t_ref[...] = lo.T.astype(BF16)
    seed_ref[...] = dot(dep_ref[...].astype(BF16), w_out_ref[...], 0, 0)
    w_in_t_ref[...] = w_in_ref[...].T
    w_mid_t_ref[...] = w_mid_ref[...].T


def main_kernel(
    far_ref, near_ref, hi_ref, lo_ref, hi_t_ref, lo_t_ref, seed_ref,
    w_in_ref, b_in_ref, w_mid_ref, b_mid_ref, w_in_t_ref, w_mid_t_ref,
    far_out_ref, near_out_ref,
):
    fetched = jnp.concatenate(
        [far_ref[...].reshape(FAR_ROWS, PAIR), near_ref[...].reshape(NEAR_PAD, PAIR)], axis=0
    )
    values = jnp.concatenate([fetched[:, :FEAT], fetched[:, WIDE : WIDE + FEAT]], axis=0)
    inputs = (dot(hi_t_ref[...], values, 1, 0) + dot(lo_t_ref[...], values, 1, 0)).astype(BF16)
    t_one = jnp.tanh(dot(inputs, w_in_ref[...], 1, 0) + b_in_ref[...])
    t_two = jnp.tanh(dot(t_one.astype(BF16), w_mid_ref[...], 1, 0) + b_mid_ref[...])
    g_two = (seed_ref[...] * (1.0 - t_two * t_two)).astype(BF16)
    g_one = (dot(g_two, w_mid_t_ref[...], 1, 0) * (1.0 - t_one * t_one)).astype(BF16)
    g_inputs = dot(g_one, w_in_t_ref[...], 1, 0)
    g_hi = g_inputs.astype(BF16)
    g_lo = (g_inputs - g_hi.astype(F32)).astype(BF16)
    slots = dot(hi_ref[...], g_hi, 1, 0) + dot(lo_ref[...], g_hi, 1, 0) + dot(hi_ref[...], g_lo, 1, 0)
    rows = jnp.concatenate(
        [
            slots[:ROWS], fetched[:, FEAT:WIDE].astype(F32),
            slots[ROWS:], fetched[:, WIDE + FEAT :].astype(F32),
        ],
        axis=1,
    ).astype(BF16)
    far_out_ref[...] = rows[:FAR_ROWS].reshape(far_out_ref.shape)
    near_out_ref[...] = rows[FAR_ROWS:].reshape(near_out_ref.shape)


def final_kernel(got_ref, out_ref):
    got = got_ref[...].reshape(-1, PAIR)
    lane = lax.broadcasted_iota(jnp.int32, (got.shape[0], QUARTER), 1).astype(F32)
    total = None
    for p in range(2):
        place = got[:, p * WIDE + FEAT : (p + 1) * WIDE].astype(F32)
        pick = jnp.where(place == lane, 1.0, 0.0).astype(BF16)
        part = dot(got[:, p * WIDE : p * WIDE + FEAT], pick, 0, 0)
        total = part if total is None else total + part
    out_ref[...] = total


def shape(dims, dtype):
    return jax.ShapeDtypeStruct(dims, dtype)


def exchange_near(near):
    moved = []
    for i in range(2 * REACH + 1):
        block = near[i * NEAR_ROWS // 2 : (i + 1) * NEAR_ROWS // 2]
        if i != REACH:
            step = i - REACH
            block = lax.ppermute(block, "dom", [(a, (a + step) % N_DOM) for a in range(N_DOM)])
        moved.append(block)
    return moved


def body(
    profiles, pack_index, obs_slot, interp_weight, departures, w_in, b_in, w_mid, b_mid, w_out
):
    dom = lax.axis_index("dom")
    dom_scalar = dom.reshape(1).astype(jnp.int32)
    smem = pl.BlockSpec(memory_space=pltpu.SMEM)
    vmem = pl.BlockSpec(memory_space=pltpu.VMEM)
    far_shape = shape((N_DOM, FAR // 2, PAIR), BF16)
    near_shape = shape((NEAR_PAD // 2, 2, PAIR), BF16)
    far, near = pl.pallas_call(
        pack_kernel,
        out_shape=(far_shape, near_shape),
        in_specs=[smem, vmem, vmem],
        scratch_shapes=[pltpu.VMEM((N_DOM, CAP), jnp.int32)],
        name="pack",
    )(dom_scalar, pack_index[0, 0].T, profiles)

    obs = obs_slot.shape[1]
    hidden = w_mid.shape[0]
    hi, lo, hi_t, lo_t, seed, w_in_t, w_mid_t = pl.pallas_call(
        prep_kernel,
        out_shape=(
            shape((2 * ROWS, obs), BF16), shape((2 * ROWS, obs), BF16),
            shape((obs, 2 * ROWS), BF16), shape((obs, 2 * ROWS), BF16),
            shape((obs, hidden), F32), shape((hidden, FEAT), BF16), shape((hidden, hidden), BF16),
        ),
        in_specs=[smem] + [vmem] * 6,
        name="prep",
    )(dom_scalar, obs_slot, interp_weight, departures, w_in, w_mid, w_out.T)

    got_far = lax.all_to_all(far, "dom", 0, 0, tiled=True)
    got_near = exchange_near(near)
    near_rows = jnp.concatenate(got_near[::-1] + [got_near[REACH][:1]], axis=0)

    far_adj, near_adj = pl.pallas_call(
        main_kernel, out_shape=(far_shape, near_shape), name="main"
    )(
        got_far, near_rows, hi, lo, hi_t, lo_t, seed,
        w_in, b_in.reshape(1, -1), w_mid, b_mid.reshape(1, -1), w_in_t, w_mid_t,
    )

    back_far = lax.all_to_all(far_adj, "dom", 0, 0, tiled=True)
    back_near = exchange_near(near_adj)[::-1]
    stacked = jnp.stack(back_near[:N_REP] * 2)
    first = lax.dynamic_slice_in_dim(stacked, (REACH - dom) % N_REP, N_REP, 0)
    owner = (jnp.arange(N_REP) == (dom + REACH) % N_REP).reshape(N_REP, 1, 1, 1)
    second = jnp.where(owner, back_near[N_REP][None], jnp.zeros((), BF16))
    by_quarter = back_far.reshape(N_DOM // N_REP, N_REP, FAR // 2, PAIR).transpose(1, 0, 2, 3)
    outgoing = jnp.concatenate([by_quarter, first, second], axis=1)
    got = lax.all_to_all(outgoing, "rep", 0, 0, tiled=True)
    return pl.pallas_call(
        final_kernel, out_shape=shape((FEAT, QUARTER), F32), name="final"
    )(got)


def solution(mesh):
    placed = (
        P(None, "dom"),
        P("dom", "rep", None, None),
        P(None, ("dom", "rep")),
        P(None, ("dom", "rep")),
        P(None, ("dom", "rep")),
        P(),
        P(),
        P(),
        P(),
        P(),
    )
    return jax.shard_map(
        body, mesh=mesh, in_specs=placed, out_specs=P(None, ("dom", "rep")), check_vma=False
    )
```

```python
import jax
import jax.numpy as jnp
from jax import lax
from jax.experimental import pallas as pl
from jax.experimental.pallas import tpu as pltpu
from jax.sharding import PartitionSpec as P


F32 = jnp.float32
BF16 = jnp.bfloat16
N_DOM = 128
N_REP = 4
CAP = 16
FAR = 4
REACH = 2
FEAT = 300
WIDE = FEAT + 1
PAIR = 2 * WIDE
FAR_ROWS = N_DOM * FAR // 2
NEAR_ROWS = (CAP - FAR) // 2
NEAR_STEP = 8
NEAR_PAD = 48
BLOCKS = 2 * REACH + 1
ROWS = FAR_ROWS + NEAR_PAD
QUARTER = 256
COLS = 1024
KERNEL_VMEM = 24 * 2**20
N_HELD = 2
N_NEARBY = 6


def dot(a, b, ca, cb):
    return lax.dot_general(a, b, (((ca,), (cb,)), ((), ())), preferred_element_type=F32)


def put_near(near_refs, rows):
    for i, ref in enumerate(near_refs):
        start = FAR_ROWS + i * NEAR_STEP
        ref[...] = rows[start : start + NEAR_STEP].reshape(ref.shape)


def pack_kernel(dom_ref, lists_ref, prof_ref, far_ref, *rest):
    near_refs, idx_ref = rest[:BLOCKS], rest[BLOCKS]
    idx = lists_ref[...].T
    idx_ref[...] = idx
    pairs = jnp.broadcast_to(idx[:, None, :], (N_DOM, FAR // 2, CAP)).reshape(FAR_ROWS, CAP)
    first = lax.broadcasted_iota(jnp.int32, (FAR_ROWS, 1), 0) % 2 == 0
    row = lax.broadcasted_iota(jnp.int32, (NEAR_PAD, CAP), 0)
    slot = lax.broadcasted_iota(jnp.int32, (NEAR_PAD, CAP), 1)
    around = jnp.zeros((NEAR_PAD, CAP), jnp.int32)
    for i in range(BLOCKS):
        other = idx_ref[pl.ds((dom_ref[0] + i + N_DOM - REACH) % N_DOM, 1), :]
        around = jnp.where(row // NEAR_STEP == i, other, around)
    around = around.astype(F32)
    prof = prof_ref[...]
    lane = lax.broadcasted_iota(jnp.int32, (ROWS, COLS), 1)
    halves = []
    for p in range(2):
        near_col = jnp.sum(
            jnp.where(slot == FAR + 2 * (row % NEAR_STEP) + p, around, 0.0), axis=1, keepdims=True
        ).astype(jnp.int32)
        far_col = jnp.where(first, pairs[:, p : p + 1], pairs[:, 2 + p : 3 + p])
        col = jnp.concatenate([far_col, near_col], axis=0)
        pick = jnp.where(col == lane, 1.0, 0.0).astype(BF16)
        halves.append(dot(pick, prof, 1, 1))
        halves.append((col % QUARTER).astype(F32))
    rows = jnp.concatenate(halves, axis=1).astype(BF16)
    far_ref[...] = rows[:FAR_ROWS].reshape(far_ref.shape)
    put_near(near_refs, rows)


def prep_kernel(
    dom_ref, slot_ref, weight_ref, dep_ref, w_out_ref,
    hi_ref, hi_t_ref, lo_t_ref, seed_ref,
):
    slot = slot_ref[...]
    owner = slot // CAP
    j = slot % CAP
    apart = (owner - dom_ref[0] + REACH) % N_DOM
    row = jnp.where(
        j < FAR, owner * (FAR // 2) + j // 2, FAR_ROWS + apart * NEAR_STEP + (j - FAR) // 2
    )
    row = row + ROWS * (j % 2)
    index = lax.broadcasted_iota(jnp.int32, (2 * ROWS, slot.shape[1]), 0)
    acc = jnp.zeros(index.shape, F32)
    for k in range(4):
        acc = acc + jnp.where(row[k : k + 1] == index, weight_ref[k : k + 1], 0.0)
    hi = acc.astype(BF16)
    lo = acc - hi.astype(F32)
    hi_ref[...] = hi
    hi_t_ref[...] = acc.T.astype(BF16)
    lo_t_ref[...] = lo.T.astype(BF16)
    seed_ref[...] = dot(dep_ref[...].astype(BF16), w_out_ref[...], 0, 0)


def main_kernel(far_ref, *refs):
    near_refs = refs[:BLOCKS]
    refs = refs[BLOCKS:]
    hi_t_ref, lo_t_ref, b_in_ref, b_mid_ref, w_in_ref, w_mid_ref = refs[:N_NEARBY]
    remote, refs = refs[N_NEARBY : N_NEARBY + N_HELD], refs[N_NEARBY + N_HELD :]
    far_out_ref, *near_out_refs = refs[: BLOCKS + 1]
    *held, sems = refs[BLOCKS + 1 :]
    copies = [pltpu.make_async_copy(a, b, sems.at[i]) for i, (a, b) in enumerate(zip(remote, held))]
    for copy in copies:
        copy.start()

    def ready(i):
        copies[i].wait()
        return held[i][...]

    parts = [far_ref[...].reshape(FAR_ROWS, PAIR)]
    parts += [ref[...].reshape(NEAR_STEP, PAIR) for ref in near_refs]
    parts += [jnp.zeros((ROWS - FAR_ROWS - BLOCKS * NEAR_STEP, PAIR), BF16)]
    fetched = jnp.concatenate(parts, axis=0)
    values = jnp.concatenate([fetched[:, :FEAT], fetched[:, WIDE : WIDE + FEAT]], axis=0)
    inputs = (dot(hi_t_ref[...], values, 1, 0) + dot(lo_t_ref[...], values, 1, 0)).astype(BF16)
    w_in = w_in_ref[...]
    t_one = jnp.tanh(dot(inputs, w_in, 1, 0) + b_in_ref[...])
    w_mid = w_mid_ref[...]
    t_two = jnp.tanh(dot(t_one.astype(BF16), w_mid, 1, 0) + b_mid_ref[...])
    g_two = (ready(0) * (1.0 - t_two * t_two)).astype(BF16)
    g_one = (dot(g_two, w_mid, 1, 1) * (1.0 - t_one * t_one)).astype(BF16)
    g_inputs = dot(g_one, w_in, 1, 1).astype(BF16)
    slots = dot(ready(1), g_inputs, 1, 0)
    rows = jnp.concatenate(
        [
            slots[:ROWS], fetched[:, FEAT:WIDE].astype(F32),
            slots[ROWS:], fetched[:, WIDE + FEAT :].astype(F32),
        ],
        axis=1,
    ).astype(BF16)
    far_out_ref[...] = rows[:FAR_ROWS].reshape(far_out_ref.shape)
    put_near(near_out_refs, rows)


def final_kernel(got_ref, out_ref):
    got = got_ref[...].reshape(-1, PAIR)
    lane = lax.broadcasted_iota(jnp.int32, (got.shape[0], QUARTER), 1).astype(F32)
    total = None
    for p in range(2):
        place = got[:, p * WIDE + FEAT : (p + 1) * WIDE].astype(F32)
        pick = jnp.where(place == lane, 1.0, 0.0).astype(BF16)
        part = dot(got[:, p * WIDE : p * WIDE + FEAT], pick, 0, 0)
        total = part if total is None else total + part
    out_ref[...] = total


def shape(dims, dtype):
    return jax.ShapeDtypeStruct(dims, dtype)


def exchange_near(near):
    moved = []
    for i, block in enumerate(near):
        if i != REACH:
            step = i - REACH
            block = lax.ppermute(block, "dom", [(a, (a + step) % N_DOM) for a in range(N_DOM)])
        moved.append(block)
    return moved


def body(
    profiles, pack_index, obs_slot, interp_weight, departures, w_in, b_in, w_mid, b_mid, w_out
):
    dom = lax.axis_index("dom")
    dom_scalar = dom.reshape(1).astype(jnp.int32)
    smem = pl.BlockSpec(memory_space=pltpu.SMEM)
    vmem = pl.BlockSpec(memory_space=pltpu.VMEM)
    far_shape = shape((N_DOM, FAR // 2, PAIR), BF16)
    near_shape = shape((NEAR_STEP // 2, 2, PAIR), BF16)
    far, *near = pl.pallas_call(
        pack_kernel,
        out_shape=(far_shape,) + (near_shape,) * BLOCKS,
        in_specs=[smem, vmem, vmem],
        scratch_shapes=[pltpu.VMEM((N_DOM, CAP), jnp.int32)],
        name="pack",
    )(dom_scalar, pack_index[0, 0].T, profiles)

    obs = obs_slot.shape[1]
    hidden = w_mid.shape[0]
    hi, hi_t, lo_t, seed = pl.pallas_call(
        prep_kernel,
        out_shape=(
            pltpu.HBM((2 * ROWS, obs), BF16), pltpu.VMEM((obs, 2 * ROWS), BF16),
            pltpu.VMEM((obs, 2 * ROWS), BF16), pltpu.HBM((obs, hidden), F32),
        ),
        in_specs=[smem] + [vmem] * 4,
        compiler_params=pltpu.CompilerParams(vmem_limit_bytes=KERNEL_VMEM),
        name="prep",
    )(dom_scalar, obs_slot, interp_weight, departures, w_out.T)

    got_far = lax.all_to_all(far, "dom", 0, 0, tiled=True)
    got_near = exchange_near(near)
    near_by = [pltpu.with_memory_space_constraint(x, pltpu.VMEM) for x in (got_far, hi_t, lo_t)]
    far_away = [pltpu.with_memory_space_constraint(x, pltpu.HBM) for x in (seed, hi)]
    far_adj, *near_adj = pl.pallas_call(
        main_kernel,
        out_shape=(pltpu.HBM(far_shape.shape, BF16),) + (near_shape,) * BLOCKS,
        in_specs=[vmem] * (1 + BLOCKS + N_NEARBY) + [pl.BlockSpec(memory_space=pltpu.HBM)] * N_HELD,
        scratch_shapes=[pltpu.VMEM(x.shape, x.dtype) for x in far_away]
        + [pltpu.SemaphoreType.DMA((N_HELD,))],
        compiler_params=pltpu.CompilerParams(vmem_limit_bytes=KERNEL_VMEM),
        name="main",
    )(
        near_by[0], *got_near[::-1], near_by[1], near_by[2],
        b_in.reshape(1, -1), b_mid.reshape(1, -1), w_in, w_mid, *far_away,
    )

    back_far = lax.all_to_all(far_adj, "dom", 0, 0, tiled=True)
    back_near = [x[: NEAR_ROWS // 2] for x in exchange_near(near_adj)[::-1]]
    stacked = jnp.stack(back_near[:N_REP] * 2)
    first = lax.dynamic_slice_in_dim(stacked, (REACH - dom) % N_REP, N_REP, 0)
    owner = (jnp.arange(N_REP) == (dom + REACH) % N_REP).reshape(N_REP, 1, 1, 1)
    second = jnp.where(owner, back_near[N_REP][None], jnp.zeros((), BF16))
    by_quarter = back_far.reshape(N_DOM // N_REP, N_REP, FAR // 2, PAIR).transpose(1, 0, 2, 3)
    outgoing = jnp.concatenate([by_quarter, first, second], axis=1)
    got = lax.all_to_all(outgoing, "rep", 0, 0, tiled=True)
    return pl.pallas_call(
        final_kernel, out_shape=shape((FEAT, QUARTER), F32), name="final"
    )(got)


def solution(mesh):
    placed = (
        P(None, "dom"),
        P("dom", "rep", None, None),
        P(None, ("dom", "rep")),
        P(None, ("dom", "rep")),
        P(None, ("dom", "rep")),
        P(),
        P(),
        P(),
        P(),
        P(),
    )
    return jax.shard_map(
        body, mesh=mesh, in_specs=placed, out_specs=P(None, ("dom", "rep")), check_vma=False
    )
```

```python
import jax
import jax.numpy as jnp
from jax import lax
from jax.experimental import pallas as pl
from jax.experimental.pallas import tpu as pltpu
from jax.sharding import PartitionSpec as P


F32 = jnp.float32
BF16 = jnp.bfloat16
N_DOM = 128
N_REP = 4
CAP = 16
FAR = 4
REACH = 2
FEAT = 300
WIDE = FEAT + 1
PAIR = 2 * WIDE
FAR_ROWS = N_DOM * FAR // 2
NEAR_ROWS = (CAP - FAR) // 2
NEAR_STEP = 8
NEAR_PAD = 48
ROWS = FAR_ROWS + NEAR_PAD
QUARTER = 256
COLS = 1024
KERNEL_VMEM = 24 * 2**20


def dot(a, b, ca, cb):
    return lax.dot_general(a, b, (((ca,), (cb,)), ((), ())), preferred_element_type=F32)


def near_rows(rows, i):
    start = FAR_ROWS + i * NEAR_STEP
    return rows[start : start + NEAR_STEP].reshape(NEAR_STEP // 2, 2, PAIR)


def pack_kernel(dom_ref, lists_ref, prof_hbm, far_ref, home_ref, swap_ref, below_ref, above_ref, idx_ref, prof_ref, sem):
    load = pltpu.make_async_copy(prof_hbm, prof_ref, sem)
    load.start()
    idx = lists_ref[...].T
    idx_ref[...] = idx
    pairs = jnp.broadcast_to(idx[:, None, :], (N_DOM, FAR // 2, CAP)).reshape(FAR_ROWS, CAP)
    first = lax.broadcasted_iota(jnp.int32, (FAR_ROWS, 1), 0) % 2 == 0
    row = lax.broadcasted_iota(jnp.int32, (NEAR_PAD, CAP), 0)
    slot = lax.broadcasted_iota(jnp.int32, (NEAR_PAD, CAP), 1)
    around = jnp.zeros((NEAR_PAD, CAP), jnp.int32)
    dom = dom_ref[0]
    toward = 1 - 2 * (dom % 2)
    for i, step in enumerate((0, toward, -toward, -REACH, REACH)):
        other = idx_ref[pl.ds((dom + step + N_DOM) % N_DOM, 1), :]
        around = jnp.where(row // NEAR_STEP == i, other, around)
    around = around.astype(F32)
    lane = lax.broadcasted_iota(jnp.int32, (ROWS, COLS), 1)
    cols, picks = [], []
    for p in range(2):
        near_col = jnp.sum(
            jnp.where(slot == FAR + 2 * (row % NEAR_STEP) + p, around, 0.0), axis=1, keepdims=True
        ).astype(jnp.int32)
        far_col = jnp.where(first, pairs[:, p : p + 1], pairs[:, 2 + p : 3 + p])
        col = jnp.concatenate([far_col, near_col], axis=0)
        cols.append((col % QUARTER).astype(F32))
        picks.append(jnp.where(col == lane, 1.0, 0.0).astype(BF16))
    load.wait()
    prof = prof_ref[...]
    rows = jnp.concatenate(
        [dot(picks[0], prof, 1, 1), cols[0], dot(picks[1], prof, 1, 1), cols[1]], axis=1
    ).astype(BF16)
    far_ref[...] = rows[:FAR_ROWS].reshape(far_ref.shape)
    home_ref[...] = near_rows(rows, 0)
    half = NEAR_STEP // 2
    swap_ref[:half] = near_rows(rows, 1)
    swap_ref[half:] = near_rows(rows, 2)
    below_ref[...] = near_rows(rows, 3)
    above_ref[...] = near_rows(rows, 4)


def prep_kernel(
    dom_ref, slot_ref, weight_ref, dep_ref, w_out_ref,
    hi_ref, hi_t_ref, lo_t_ref, seed_ref,
):
    slot = slot_ref[...]
    owner = slot // CAP
    j = slot % CAP
    dom = dom_ref[0]
    odd = dom % 2
    apart = (owner - dom + REACH) % N_DOM
    block = jnp.where(apart == REACH, 0, jnp.where(apart == 2 * REACH, 2, 3))
    block = jnp.where(apart == REACH + 1, 1 + 3 * odd, block)
    block = jnp.where(apart == REACH - 1, 5 - 4 * odd, block)
    row = jnp.where(
        j < FAR, owner * (FAR // 2) + j // 2, FAR_ROWS + block * NEAR_STEP + (j - FAR) // 2
    )
    row = row + ROWS * (j % 2)
    index = lax.broadcasted_iota(jnp.int32, (2 * ROWS, slot.shape[1]), 0)
    acc = jnp.zeros(index.shape, F32)
    for k in range(4):
        acc = acc + jnp.where(row[k : k + 1] == index, weight_ref[k : k + 1], 0.0)
    hi = acc.astype(BF16)
    lo = acc - hi.astype(F32)
    hi_ref[...] = hi
    hi_t_ref[...] = acc.T.astype(BF16)
    lo_t_ref[...] = lo.T.astype(BF16)
    seed_ref[...] = dot(dep_ref[...].astype(BF16), w_out_ref[...], 0, 0)


def main_kernel(
    dom_ref, far_ref, home_ref, swap_ref, down_ref, up_ref,
    hi_t_ref, lo_t_ref, b_in_ref, b_mid_ref, w_in_ref, w_mid_ref, seed_hbm, hi_hbm,
    far_out_ref, home_out_ref, swap_out_ref, below_out_ref, above_out_ref,
    seed_ref, hi_ref, sems,
):
    remote, held = (seed_hbm, hi_hbm), (seed_ref, hi_ref)
    copies = [pltpu.make_async_copy(a, b, sems.at[i]) for i, (a, b) in enumerate(zip(remote, held))]
    for copy in copies:
        copy.start()

    def ready(i):
        copies[i].wait()
        return held[i][...]

    half = NEAR_STEP // 2
    near = (home_ref[...], swap_ref[:half], down_ref[:half], up_ref[:half], down_ref[half:], up_ref[half:])
    parts = [far_ref[...].reshape(FAR_ROWS, PAIR)]
    parts += [x.reshape(NEAR_STEP, PAIR) for x in near]
    fetched = jnp.concatenate(parts, axis=0)
    values = jnp.concatenate([fetched[:, :FEAT], fetched[:, WIDE : WIDE + FEAT]], axis=0)
    inputs = (dot(hi_t_ref[...], values, 1, 0) + dot(lo_t_ref[...], values, 1, 0)).astype(BF16)
    w_in = w_in_ref[...]
    t_one = jnp.tanh(dot(inputs, w_in, 1, 0) + b_in_ref[...])
    w_mid = w_mid_ref[...]
    t_two = jnp.tanh(dot(t_one.astype(BF16), w_mid, 1, 0) + b_mid_ref[...])
    g_two = (ready(0) * (1.0 - t_two * t_two)).astype(BF16)
    g_one = (dot(g_two, w_mid, 1, 1) * (1.0 - t_one * t_one)).astype(BF16)
    g_inputs = dot(g_one, w_in, 1, 1).astype(BF16)
    slots = dot(ready(1), g_inputs, 1, 0)
    rows = jnp.concatenate(
        [
            slots[:ROWS], fetched[:, FEAT:WIDE].astype(F32),
            slots[ROWS:], fetched[:, WIDE + FEAT :].astype(F32),
        ],
        axis=1,
    ).astype(BF16)
    far_out_ref[...] = rows[:FAR_ROWS].reshape(far_out_ref.shape)
    odd = dom_ref[0] % 2 == 1
    home_out_ref[...] = near_rows(rows, 0)
    swap_out_ref[:half] = near_rows(rows, 1)
    swap_out_ref[half:] = jnp.where(odd, near_rows(rows, 4), near_rows(rows, 5))
    below_out_ref[...] = near_rows(rows, 3)
    above_out_ref[...] = near_rows(rows, 2)


def final_kernel(got_ref, out_ref):
    got = got_ref[...].reshape(-1, PAIR)
    lane = lax.broadcasted_iota(jnp.int32, (got.shape[0], QUARTER), 1).astype(F32)
    total = None
    for p in range(2):
        place = got[:, p * WIDE + FEAT : (p + 1) * WIDE].astype(F32)
        pick = jnp.where(place == lane, 1.0, 0.0).astype(BF16)
        part = dot(got[:, p * WIDE : p * WIDE + FEAT], pick, 0, 0)
        total = part if total is None else total + part
    out_ref[...] = total


def shape(dims, dtype):
    return jax.ShapeDtypeStruct(dims, dtype)


def exchange_near(swap, below, above):
    half = NEAR_STEP // 2
    swapped = lax.ppermute(swap, "dom", [(a, a ^ 1) for a in range(N_DOM)])
    moved = [swapped]
    for block, step in ((below, -REACH), (above, REACH)):
        both = jnp.concatenate([block, swapped[half:]], axis=0)
        moved.append(lax.ppermute(both, "dom", [(a, (a + step) % N_DOM) for a in range(N_DOM)]))
    return moved


def body(
    profiles, pack_index, obs_slot, interp_weight, departures, w_in, b_in, w_mid, b_mid, w_out
):
    dom = lax.axis_index("dom")
    dom_scalar = dom.reshape(1).astype(jnp.int32)
    smem = pl.BlockSpec(memory_space=pltpu.SMEM)
    vmem = pl.BlockSpec(memory_space=pltpu.VMEM)
    far_dims = (N_DOM, FAR // 2, PAIR)
    one_dims, two_dims = (NEAR_STEP // 2, 2, PAIR), (NEAR_STEP, 2, PAIR)
    packed_shapes = tuple(pltpu.HBM(x, BF16) for x in (far_dims, one_dims, two_dims, one_dims, one_dims))
    hbm = pl.BlockSpec(memory_space=pltpu.HBM)
    far, home, swap, below, above = pl.pallas_call(
        pack_kernel,
        out_shape=packed_shapes,
        in_specs=[smem, vmem, hbm],
        scratch_shapes=[
            pltpu.VMEM((N_DOM, CAP), jnp.int32), pltpu.VMEM(profiles.shape, BF16), pltpu.SemaphoreType.DMA,
        ],
        name="pack",
    )(dom_scalar, pack_index[0, 0].T, profiles)

    obs = obs_slot.shape[1]
    hidden = w_mid.shape[0]
    hi, hi_t, lo_t, seed = pl.pallas_call(
        prep_kernel,
        out_shape=(
            pltpu.HBM((2 * ROWS, obs), BF16), pltpu.VMEM((obs, 2 * ROWS), BF16),
            pltpu.VMEM((obs, 2 * ROWS), BF16), pltpu.HBM((obs, hidden), F32),
        ),
        in_specs=[smem] + [vmem] * 4,
        compiler_params=pltpu.CompilerParams(vmem_limit_bytes=KERNEL_VMEM),
        name="prep",
    )(dom_scalar, obs_slot, interp_weight, departures, w_out.T)

    got_far = lax.all_to_all(far, "dom", 0, 0, tiled=True)
    got_near = exchange_near(swap, below, above)
    near_by = [pltpu.with_memory_space_constraint(x, pltpu.VMEM) for x in (got_far, hi_t, lo_t)]
    far_away = [pltpu.with_memory_space_constraint(x, pltpu.HBM) for x in (seed, hi)]
    far_adj, home_adj, swap_adj, below_adj, above_adj = pl.pallas_call(
        main_kernel,
        out_shape=packed_shapes,
        in_specs=[smem] + [vmem] * 11 + [hbm] * 2,
        scratch_shapes=[pltpu.VMEM(x.shape, x.dtype) for x in (seed, hi)]
        + [pltpu.SemaphoreType.DMA((2,))],
        compiler_params=pltpu.CompilerParams(vmem_limit_bytes=KERNEL_VMEM),
        name="main",
    )(
        dom_scalar, near_by[0], home, *got_near, near_by[1], near_by[2],
        b_in.reshape(1, -1), b_mid.reshape(1, -1), w_in, w_mid, *far_away,
    )

    back_far = lax.all_to_all(far_adj, "dom", 0, 0, tiled=True)
    swapped, down, up = exchange_near(swap_adj, below_adj, above_adj)
    half, kept = NEAR_STEP // 2, NEAR_ROWS // 2
    relayed = jnp.where(dom % 2 == 1, down[half : half + kept], up[half : half + kept])
    blocks = [home_adj[:kept], swapped[:kept], down[:kept], relayed]
    blocks = [jnp.where(dom % 2 == 1, blocks[i ^ 1], blocks[i]) for i in range(N_REP)]
    first = jnp.stack([jnp.where(dom % 4 >= 2, blocks[i ^ 2], blocks[i]) for i in range(N_REP)])
    owner = (jnp.arange(N_REP) == (dom + REACH) % N_REP).reshape(N_REP, 1, 1, 1)
    second = jnp.where(owner, up[:kept][None], jnp.zeros((), BF16))
    by_quarter = back_far.reshape(N_DOM // N_REP, N_REP, FAR // 2, PAIR).transpose(1, 0, 2, 3)
    outgoing = jnp.concatenate([by_quarter, first, second], axis=1)
    got = lax.all_to_all(outgoing, "rep", 0, 0, tiled=True)
    return pl.pallas_call(
        final_kernel, out_shape=shape((FEAT, QUARTER), F32), name="final"
    )(pltpu.with_memory_space_constraint(got, pltpu.VMEM))


def solution(mesh):
    placed = (
        P(None, "dom"),
        P("dom", "rep", None, None),
        P(None, ("dom", "rep")),
        P(None, ("dom", "rep")),
        P(None, ("dom", "rep")),
        P(),
        P(),
        P(),
        P(),
        P(),
    )
    return jax.shard_map(
        body, mesh=mesh, in_specs=placed, out_specs=P(None, ("dom", "rep")), check_vma=False
    )
```

```python
import jax
import jax.numpy as jnp
from jax import lax
from jax.experimental import pallas as pl
from jax.experimental.pallas import tpu as pltpu
from jax.sharding import Mesh, PartitionSpec as P


DOM = ("m", "q")
BY_QUARTER = ("q", "m")
F32 = jnp.float32
BF16 = jnp.bfloat16
N_DOM = 128
N_REP = 4
CAP = 16
FAR = 4
REACH = 2
FEAT = 300
WIDE = FEAT + 1
PAIR = 2 * WIDE
FAR_ROWS = N_DOM * FAR // 2
NEAR_ROWS = (CAP - FAR) // 2
NEAR_STEP = 8
NEAR_PAD = 48
ROWS = FAR_ROWS + NEAR_PAD
QUARTER = 256
QUARTER_ROWS = FAR_ROWS // N_REP
KERNEL_VMEM = 24 * 2**20


def dot(a, b, ca, cb):
    return lax.dot_general(a, b, (((ca,), (cb,)), ((), ())), preferred_element_type=F32)


def near_rows(rows, i):
    start = i * NEAR_STEP
    return rows[start : start + NEAR_STEP].reshape(NEAR_STEP // 2, 2, PAIR)


def pack_kernel(dom_ref, lists_ref, prof_hbm, far_ref, home_ref, swap_ref, below_ref, above_ref, idx_ref, prof_ref, sem):
    load = pltpu.make_async_copy(prof_hbm, prof_ref, sem)
    load.start()
    idx = lists_ref[...].T
    idx_ref[...] = idx
    row = lax.broadcasted_iota(jnp.int32, (NEAR_PAD, CAP), 0)
    slot = lax.broadcasted_iota(jnp.int32, (NEAR_PAD, CAP), 1)
    around = jnp.zeros((NEAR_PAD, CAP), jnp.int32)
    dom = dom_ref[0]
    toward = 1 - 2 * (dom % 2)
    for i, step in enumerate((0, toward, -toward, -REACH, REACH)):
        other = idx_ref[pl.ds((dom + step + N_DOM) % N_DOM, 1), :]
        around = jnp.where(row // NEAR_STEP == i, other, around)
    around = around.astype(F32)
    lane = lax.broadcasted_iota(jnp.int32, (1, QUARTER), 1).astype(F32).astype(BF16)
    one, zero = jnp.ones((), BF16), jnp.zeros((), BF16)
    near_col = jnp.concatenate(
        [
            jnp.sum(jnp.where(slot == FAR + 2 * (row % NEAR_STEP) + p, around, 0.0), axis=1, keepdims=True)
            for p in range(2)
        ],
        axis=0,
    ).astype(jnp.int32)
    near_place = (near_col % QUARTER).astype(F32)
    first = lax.broadcasted_iota(jnp.int32, (QUARTER_ROWS, 1), 0) % 2 == 0
    places, picks = [], []
    for q in range(N_REP):
        part = idx_ref[pl.ds(q, N_DOM // N_REP, stride=N_REP), :]
        part = jnp.broadcast_to(part[:, None, :], (N_DOM // N_REP, FAR // 2, CAP)).reshape(QUARTER_ROWS, CAP)
        col = jnp.concatenate(
            [jnp.where(first, part[:, p : p + 1], part[:, 2 + p : 3 + p]) for p in range(2)], axis=0
        )
        place = (col % QUARTER).astype(F32)
        here = jnp.where(near_col // QUARTER == q, near_place, -1.0)
        both = jnp.concatenate([place, here], axis=0).astype(BF16)
        places.append(place)
        picks.append(jnp.where(both == lane, one, zero))
    load.wait()
    near = None
    for q in range(N_REP):
        out = dot(picks[q], prof_ref[:, q * QUARTER : (q + 1) * QUARTER], 1, 1)
        n, place = QUARTER_ROWS, places[q]
        rows = jnp.concatenate([out[:n], place[:n], out[n : 2 * n], place[n:]], axis=1).astype(BF16)
        m = N_DOM // N_REP
        far_ref[q * m : (q + 1) * m] = rows.reshape(m, FAR // 2, PAIR)
        near = out[2 * n :] if near is None else near + out[2 * n :]
    n = NEAR_PAD
    rows = jnp.concatenate([near[:n], near_place[:n], near[n:], near_place[n:]], axis=1).astype(BF16)
    half = NEAR_STEP // 2
    home_ref[...] = near_rows(rows, 0)
    swap_ref[:half] = near_rows(rows, 1)
    swap_ref[half:] = near_rows(rows, 2)
    below_ref[...] = near_rows(rows, 3)
    above_ref[...] = near_rows(rows, 4)


def prep_kernel(
    dom_ref, slot_ref, weight_ref, dep_ref, w_out_ref, b_in_ref, b_mid_ref,
    hi_ref, both_t_ref, seed_ref, b_in_out_ref, b_mid_out_ref,
):
    slot = slot_ref[...]
    owner = slot // CAP
    j = slot % CAP
    dom = dom_ref[0]
    odd = dom % 2
    apart = (owner - dom + REACH) % N_DOM
    block = jnp.where(apart == REACH, 0, jnp.where(apart == 2 * REACH, 2, 3))
    block = jnp.where(apart == REACH + 1, 1 + 3 * odd, block)
    block = jnp.where(apart == REACH - 1, 5 - 4 * odd, block)
    place = owner % N_REP * (N_DOM // N_REP) + owner // N_REP
    row = jnp.where(
        j < FAR, place * (FAR // 2) + j // 2, FAR_ROWS + block * NEAR_STEP + (j - FAR) // 2
    )
    row = row + ROWS * (j % 2)
    index = lax.broadcasted_iota(jnp.int32, (2 * ROWS, slot.shape[1]), 0)
    acc = jnp.zeros(index.shape, F32)
    for k in range(4):
        acc = acc + jnp.where(row[k : k + 1] == index, weight_ref[k : k + 1], 0.0)
    hi = acc.astype(BF16)
    lo = acc - hi.astype(F32)
    hi_ref[...] = hi
    both_t_ref[...] = jnp.concatenate([acc.T, lo.T], axis=1).astype(BF16)
    b_in_out_ref[...] = b_in_ref[...]
    b_mid_out_ref[...] = b_mid_ref[...]
    seed_ref[...] = dot(dep_ref[...].astype(BF16), w_out_ref[...], 0, 0)


def main_kernel(
    dom_ref, far_ref, home_ref, swap_ref, down_ref, up_ref,
    both_t_ref, b_in_ref, b_mid_ref, w_in_ref, w_mid_ref, seed_hbm, hi_hbm,
    far_out_ref, home_out_ref, swap_out_ref, below_out_ref, above_out_ref,
    seed_ref, hi_ref, sems,
):
    remote, held = (seed_hbm, hi_hbm), (seed_ref, hi_ref)
    copies = [pltpu.make_async_copy(a, b, sems.at[i]) for i, (a, b) in enumerate(zip(remote, held))]
    for copy in copies:
        copy.start()

    def ready(i):
        copies[i].wait()
        return held[i][...]

    half = NEAR_STEP // 2
    near = (home_ref[...], swap_ref[:half], down_ref[:half], up_ref[:half], down_ref[half:], up_ref[half:])
    parts = [far_ref[...].reshape(FAR_ROWS, PAIR)]
    parts += [x.reshape(NEAR_STEP, PAIR) for x in near]
    fetched = jnp.concatenate(parts, axis=0)
    values = [fetched[:, :FEAT], fetched[:, WIDE : WIDE + FEAT]] * 2
    inputs = dot(both_t_ref[...], jnp.concatenate(values, axis=0), 1, 0).astype(BF16)
    w_in = w_in_ref[...]
    t_one = jnp.tanh(dot(inputs, w_in, 1, 0) + b_in_ref[...])
    w_mid = w_mid_ref[...]
    t_two = jnp.tanh(dot(t_one.astype(BF16), w_mid, 1, 0) + b_mid_ref[...])
    g_two = (ready(0) * (1.0 - t_two * t_two)).astype(BF16)
    g_one = (dot(g_two, w_mid, 1, 1) * (1.0 - t_one * t_one)).astype(BF16)
    g_inputs = dot(g_one, w_in, 1, 1).astype(BF16)
    slots = dot(ready(1), g_inputs, 1, 0)
    rows = jnp.concatenate(
        [
            slots[:ROWS], fetched[:, FEAT:WIDE].astype(F32),
            slots[ROWS:], fetched[:, WIDE + FEAT :].astype(F32),
        ],
        axis=1,
    ).astype(BF16)
    far_out_ref[...] = rows[:FAR_ROWS].reshape(far_out_ref.shape)
    rows = rows[FAR_ROWS:]
    odd = dom_ref[0] % 2 == 1
    home_out_ref[...] = near_rows(rows, 0)
    swap_out_ref[:half] = near_rows(rows, 1)
    swap_out_ref[half:] = jnp.where(odd, near_rows(rows, 4), near_rows(rows, 5))
    below_out_ref[...] = near_rows(rows, 3)
    above_out_ref[...] = near_rows(rows, 2)


def final_kernel(got_ref, out_ref):
    got = got_ref[...].reshape(-1, PAIR)
    lane = lax.broadcasted_iota(jnp.int32, (1, QUARTER), 1).astype(F32).astype(BF16)
    one, zero = jnp.ones((), BF16), jnp.zeros((), BF16)
    total = None
    for p in range(2):
        place = got[:, p * WIDE + FEAT : (p + 1) * WIDE]
        pick = jnp.where(place == lane, one, zero)
        part = dot(got[:, p * WIDE : p * WIDE + FEAT], pick, 0, 0)
        total = part if total is None else total + part
    out_ref[...] = total


def shape(dims, dtype):
    return jax.ShapeDtypeStruct(dims, dtype)


def exchange_near(swap, below, above):
    half = NEAR_STEP // 2
    swapped = lax.ppermute(swap, DOM, [(a, a ^ 1) for a in range(N_DOM)])
    moved = [swapped]
    for block, step in ((below, -REACH), (above, REACH)):
        both = jnp.concatenate([block, swapped[half:]], axis=0)
        moved.append(lax.ppermute(both, DOM, [(a, (a + step) % N_DOM) for a in range(N_DOM)]))
    return moved


def body(
    profiles, pack_index, obs_slot, interp_weight, departures, w_in, b_in, w_mid, b_mid, w_out
):
    dom = lax.axis_index(DOM)
    dom_scalar = dom.reshape(1).astype(jnp.int32)
    smem = pl.BlockSpec(memory_space=pltpu.SMEM)
    vmem = pl.BlockSpec(memory_space=pltpu.VMEM)
    far_dims = (N_DOM, FAR // 2, PAIR)
    one_dims, two_dims = (NEAR_STEP // 2, 2, PAIR), (NEAR_STEP, 2, PAIR)
    packed_shapes = (
        pltpu.HBM(far_dims, BF16), pltpu.VMEM(one_dims, BF16), pltpu.HBM(two_dims, BF16),
        pltpu.HBM(one_dims, BF16), pltpu.HBM(one_dims, BF16),
    )
    hbm = pl.BlockSpec(memory_space=pltpu.HBM)
    far, home, swap, below, above = pl.pallas_call(
        pack_kernel,
        out_shape=packed_shapes,
        in_specs=[smem, vmem, hbm],
        scratch_shapes=[
            pltpu.VMEM((N_DOM, CAP), jnp.int32), pltpu.VMEM(profiles.shape, BF16), pltpu.SemaphoreType.DMA,
        ],
        name="pack",
    )(dom_scalar, pack_index[0, 0].T, profiles)

    obs = obs_slot.shape[1]
    hidden = w_mid.shape[0]
    hi, both_t, seed, bias_in, bias_mid = pl.pallas_call(
        prep_kernel,
        out_shape=(
            pltpu.HBM((2 * ROWS, obs), BF16), pltpu.VMEM((obs, 4 * ROWS), BF16),
            pltpu.HBM((obs, hidden), F32),
            pltpu.VMEM((1, hidden), F32), pltpu.VMEM((1, hidden), F32),
        ),
        in_specs=[smem] + [vmem] * 6,
        compiler_params=pltpu.CompilerParams(vmem_limit_bytes=KERNEL_VMEM),
        name="prep",
    )(
        dom_scalar, obs_slot, interp_weight, departures, w_out.T,
        b_in.reshape(1, -1), b_mid.reshape(1, -1),
    )

    got_far = lax.all_to_all(far, BY_QUARTER, 0, 0, tiled=True)
    got_near = exchange_near(swap, below, above)
    near_by = [
        pltpu.with_memory_space_constraint(x, pltpu.VMEM)
        for x in (got_far, home, both_t, bias_in, bias_mid)
    ]
    far_away = [pltpu.with_memory_space_constraint(x, pltpu.HBM) for x in (seed, hi)]
    far_adj, home_adj, swap_adj, below_adj, above_adj = pl.pallas_call(
        main_kernel,
        out_shape=packed_shapes,
        in_specs=[smem] + [vmem] * 10 + [hbm] * 2,
        scratch_shapes=[pltpu.VMEM(x.shape, x.dtype) for x in (seed, hi)]
        + [pltpu.SemaphoreType.DMA((2,))],
        compiler_params=pltpu.CompilerParams(vmem_limit_bytes=KERNEL_VMEM),
        name="main",
    )(
        dom_scalar, *near_by[:2], *got_near, *near_by[2:], w_in, w_mid, *far_away,
    )

    back_far = lax.all_to_all(far_adj, BY_QUARTER, 0, 0, tiled=True)
    swapped, down, up = exchange_near(swap_adj, below_adj, above_adj)
    half, kept = NEAR_STEP // 2, NEAR_ROWS // 2
    relayed = jnp.where(dom % 2 == 1, down[half : half + kept], up[half : half + kept])
    blocks = [home_adj[:kept], swapped[:kept], down[:kept], relayed]
    blocks = [jnp.where(dom % 2 == 1, blocks[i ^ 1], blocks[i]) for i in range(N_REP)]
    first = jnp.stack([jnp.where(dom % 4 >= 2, blocks[i ^ 2], blocks[i]) for i in range(N_REP)])
    owner = (jnp.arange(N_REP) == (dom + REACH) % N_REP).reshape(N_REP, 1, 1, 1)
    second = jnp.where(owner, up[:kept][None], jnp.zeros((), BF16))
    by_quarter = back_far.reshape(N_REP, N_DOM // N_REP, FAR // 2, PAIR)
    outgoing = jnp.concatenate([by_quarter, first, second], axis=1)
    got = lax.all_to_all(outgoing, "rep", 0, 0, tiled=True)
    return pl.pallas_call(
        final_kernel, out_shape=shape((FEAT, QUARTER), F32), name="final"
    )(pltpu.with_memory_space_constraint(got, pltpu.VMEM))


def solution(mesh):
    cut = Mesh(mesh.devices.reshape(N_DOM // N_REP, N_REP, N_REP), DOM + ("rep",))
    all_axes = DOM + ("rep",)
    placed = (
        P(None, DOM),
        P(DOM, "rep", None, None),
        P(None, all_axes),
        P(None, all_axes),
        P(None, all_axes),
        P(),
        P(),
        P(),
        P(),
        P(),
    )
    return jax.shard_map(body, mesh=cut, in_specs=placed, out_specs=P(None, all_axes), check_vma=False)
```
